32 devices in a mesh: row: 4 (over y, core), col: 8 (over z, x).
Axes of the slice: x: 2, y: 2, z: 4, core: 2. Of those that a mesh axis runs over, the one named last changes fastest.
Arguments:
- amplitudes: float32 [1024, 1024], P('row', 'col'), may hold values from -8 to 8, as said below
- factors: float32 [1024, 1536], P(('row', 'col')), may hold values from -1.5 to 1.5
- occ_map: int32 [1024], P(('row', 'col')), may hold values from 0 to 127
- vir_map: int32 [1024], P(('row', 'col')), may hold values from 0 to 1023
- occ_energy: float32 [128], replicated, may hold values from -2 to -0.3
- vir_energy: float32 [1024], replicated, may hold values from 0.2 to 3
Outputs:
- new_amplitudes: float32 [1024, 1024], P('row', 'col')
- density: float32 [1024, 1536], P('row', 'col')
The draws below stay inside these ranges and needn't reach their ends.
Inputs may be any that keep to these rules, and one draw needn't show every extreme that they name: amplitudes equals its transpose, up to float32 rounding.
All inputs are finite; a program needn't handle non-finite values.
Results may differ from the reference program's by a relative error of at most 0.00012.
Values sent between devices are 32-bit elements; how exact they have to be, the bound alone decides.
A program may use at most 64 MiB of HBM per device.

```python
import jax
import jax.numpy as jnp
from jax import lax

NAUX = 1536
NOCC = 128
NVIR = 1024
NW = 1024
TR = 256
N_ROW = 4


def draw_amplitudes(key, part):
    base = jax.random.truncated_normal(key, -4.0, 4.0, (NW, NW), jnp.float32)
    sym = (base + base.T) * 0.5 ** 0.5 / NW ** 0.5
    return jnp.clip(sym, -8.0, 8.0)


def plant(result, stream_key, smallest, high):
    longest = result.shape.index(max(result.shape))
    spots = []
    for shift in (0, 1):
        where = [jax.random.randint(jax.random.fold_in(stream_key, axis), (), 0, length) for axis, length in enumerate(result.shape)]
        where[longest] = (where[longest] + shift) % result.shape[longest]
        spots.append(tuple(where))
    return result.at[spots[0]].set(smallest).at[spots[1]].set(high)


def block_levels(key, shape, pieces, low, high):
    loudness = 1.0
    for axis_at, parts in pieces:
        steps = jax.random.uniform(jax.random.fold_in(jax.random.fold_in(key, 6), axis_at), (parts,), jnp.float32, low / len(pieces), high / len(pieces))
        loudness = loudness * jnp.repeat(jnp.exp(steps), shape[axis_at] // parts).reshape((-1,) + (1,) * (len(shape) - 1 - axis_at))
    return loudness


def bell_draw(own_key, extent, scale, reach, split=(), dtype=jnp.bfloat16):
    level = block_levels(own_key, extent, split, -0.22, 0.18) if split else 1.0
    array = jax.random.normal(own_key, extent, jnp.float32) * scale * level
    return jnp.minimum(jnp.maximum(array, -reach), reach).astype(dtype)


def setup_inputs(seed: int = 0) -> dict:
    seeds = jax.random.split(jax.random.key(seed), 7)
    return {
        "amplitudes": draw_amplitudes(jax.random.fold_in(seeds[6], 71), 0),
        "factors": bell_draw(seeds[1], (NW, NAUX), 0.25, 1.5, ((0, 32),), jnp.float32),
        "occ_map": plant(jax.random.randint(seeds[2], (NW,), 0, NOCC), jax.random.fold_in(seeds[2], 1), 0, NOCC - 1).astype(jnp.int32),
        "vir_map": plant(jax.random.randint(seeds[3], (NW,), 0, NVIR), jax.random.fold_in(seeds[3], 1), 0, NVIR - 1).astype(jnp.int32),
        "occ_energy": jnp.clip(jax.random.uniform(seeds[4], (NOCC,), jnp.float32, -2.0, -0.3), -2.0, -0.3),
        "vir_energy": jnp.clip(jax.random.uniform(seeds[5], (NVIR,), jnp.float32, 0.2, 3.0), 0.2, 3.0),
    }


HIGHEST = lax.Precision.HIGHEST


def reference(amplitudes, factors, occ_map, vir_map, occ_energy, vir_energy):
    pair_energy = vir_energy[vir_map] - occ_energy[occ_map]
    mixed = jnp.dot(amplitudes, factors, precision=HIGHEST, preferred_element_type=jnp.float32)
    left_side = factors + mixed

    def one_block(block):
        left_rows, factor_rows, mixed_rows, energy_rows = block
        residual = jnp.dot(left_rows, factors.T, precision=HIGHEST, preferred_element_type=jnp.float32)
        residual = residual + jnp.dot(factor_rows, mixed.T, precision=HIGHEST, preferred_element_type=jnp.float32)
        new_amp = -residual / (energy_rows[:, None] + pair_energy[None, :])
        dens_rows = jnp.dot(new_amp, factors, precision=HIGHEST, preferred_element_type=jnp.float32)
        return new_amp, dens_rows

    new_amp, dens_rows = lax.map(one_block, (left_side.reshape(N_ROW, TR, NAUX), factors.reshape(N_ROW, TR, NAUX), mixed.reshape(N_ROW, TR, NAUX), pair_energy.reshape(N_ROW, TR)))
    return new_amp.reshape(NW, NW), dens_rows.reshape(NW, NAUX)
```

```python
import functools

import jax
import jax.numpy as jnp
from jax import lax
from jax.experimental import pallas as pl
from jax.experimental.pallas import tpu as pltpu
from jax.sharding import PartitionSpec as P

HIGHEST = lax.Precision.HIGHEST
MESH = pl.DeviceIdType.MESH
LANES = 128
SUB = 8


def spread(x, axis, root):
    mine = lax.axis_index(axis) == root
    return lax.psum(jnp.where(mine, x, jnp.zeros_like(x)), axis)


def pair_energies(occ_map, vir_map, occ_energy, vir_energy):
    def pick(index, table):
        hot = index[:, None] == jnp.arange(table.shape[0], dtype=jnp.int32)[None, :]
        return jnp.sum(jnp.where(hot, table[None, :], 0.0), axis=1)

    return pick(vir_map, vir_energy) - pick(occ_map, occ_energy)


def general(amplitudes, factors, occ_map, vir_map, occ_energy, vir_energy):
    col_ratio = lax.axis_size("col") // lax.axis_size("row")
    column = lax.axis_index("col")
    pair_energy = pair_energies(occ_map, vir_map, occ_energy, vir_energy)
    row_factor, row_energy = (
        lax.all_gather(factors, "col", axis=0, tiled=True),
        lax.all_gather(pair_energy, "col", axis=0, tiled=True),
    )
    tile_width = amplitudes.shape[1]
    offset = column % col_ratio * tile_width
    source = column // col_ratio
    col_factor, col_energy = (
        spread(lax.dynamic_slice_in_dim(row_factor, offset, tile_width, 0), "row", source),
        spread(lax.dynamic_slice_in_dim(row_energy, offset, tile_width, 0), "row", source),
    )
    mixed_rows = lax.psum(
        jnp.dot(amplitudes, col_factor, precision=HIGHEST, preferred_element_type=jnp.float32),
        "col",
    )
    transposed = lax.dot_general(
        amplitudes,
        row_factor,
        (((0,), (0,)), ((), ())),
        precision=HIGHEST,
        preferred_element_type=jnp.float32,
    )
    mixed_cols = lax.psum(transposed, "row")
    contract = (((1,), (1,)), ((), ()))
    residual = lax.dot_general(
        row_factor + mixed_rows,
        col_factor,
        contract,
        precision=HIGHEST,
        preferred_element_type=jnp.float32,
    )
    residual = residual + lax.dot_general(
        row_factor, mixed_cols, contract, precision=HIGHEST, preferred_element_type=jnp.float32
    )
    new_amp = -residual / (row_energy[:, None] + col_energy[None, :])
    dens_terms = jnp.dot(new_amp, col_factor, precision=HIGHEST, preferred_element_type=jnp.float32)
    density = lax.psum_scatter(dens_terms, "col", scatter_dimension=1, tiled=True)
    return (new_amp, density)


def halves(v):
    high = v.astype(jnp.bfloat16)
    return high, (v - high.astype(jnp.float32)).astype(jnp.bfloat16)


def dot3(a, b, dims):
    (ah, al), (bh, bl) = a, b
    dot = functools.partial(
        lax.dot_general, dimension_numbers=(dims, ((), ())), preferred_element_type=jnp.float32
    )
    return dot(ah, bh) + (dot(ah, bl) + dot(al, bh))


NN = ((1,), (0,))
NT = ((1,), (1,))


def kernel(
    n_row, ratio, own, width,
    f_ref, a_ref, om_ref, vm_ref, oe_ref, ve_ref, t_ref, o_ref,
    fp, pv, pb, fb, fh, fl, ab, sp, sr1, sp2, sr2, st, xr, tb, mx, db,
    f1s, f1r, pvs, pvr, zs, zr, as_, ar, ps, pr, s1s, s1r, s2s, s2r, xs, xrs,
    ts, tr, us, ur, ds_, dr,
):
    n_z = n_row
    r = lax.axis_index("row")
    c = lax.axis_index("col")
    z, x = c // ratio, c % ratio
    k = r % 2
    h = r // 2
    mate = r + 1 - 2 * k
    n_h = n_row // 2
    rows, cols = a_ref.shape
    half = own // 2
    rest = width - LANES
    me = r * ratio + x

    def part_of(row):
        return (row % 2) * n_h + row // 2

    goal = part_of(r)
    stays = (r == z) & (goal == z)

    def copy(src, dst, send, recv, row, col):
        return pltpu.make_async_remote_copy(
            src_ref=src, dst_ref=dst, send_sem=send, recv_sem=recv,
            device_id=(row, col), device_id_type=MESH,
        )

    def arrived(buf, recv):
        copy(buf, buf, ds_.at[0], recv, mate, c).wait_recv()

    def greet(row, col):
        pl.semaphore_signal(
            pltpu.get_barrier_semaphore(), inc=1, device_id=(row, col), device_id_type=MESH
        )

    def place(dh, dx, dk):
        return ((h + dh) % n_h) * 2 + (k + dk) % 2, (x + dx) % ratio

    group8 = [(dh, dx, dk) for dh in range(n_h) for dx in range(ratio) for dk in range(2)]
    plane = group8[1:]
    peers = [(dh, dx) for dh in range(n_h) for dx in range(ratio) if dh or dx]

    for off in plane:
        row, xx = place(*off)
        greet(row, z * ratio + xx)

    @pl.when(z > 0)
    def _():
        greet(r, c - ratio)

    @pl.when(z < n_z - 1)
    def _():
        greet(r, c + ratio)

    for p in range(n_row * ratio):
        fp[p, :own] = f_ref[:, p * width:p * width + LANES]
        tail = f_ref[:, p * width + LANES:(p + 1) * width]
        fp[p, own:] = jnp.concatenate([tail[:half], tail[half:]], axis=1)
    fb[r, z, x] = fp[goal * ratio + x]

    def pick(index_ref, table_ref):
        size = table_ref.shape[1]
        index = jnp.broadcast_to(index_ref[...].astype(jnp.float32), (own, own))
        diag = lax.broadcasted_iota(jnp.int32, (own, own), 0) == lax.broadcasted_iota(jnp.int32, (own, own), 1)
        column = jnp.sum(jnp.where(diag, index, 0.0), axis=1, keepdims=True)
        spot = lax.broadcasted_iota(jnp.int32, (own, size), 1).astype(jnp.float32)
        table = jnp.broadcast_to(table_ref[...], (own, size))
        return jnp.sum(jnp.where(spot == column, table, 0.0), axis=1, keepdims=True)

    pe = pick(vm_ref, ve_ref) - pick(om_ref, oe_ref)
    turn = lax.broadcasted_iota(jnp.int32, (own, LANES), 0) == lax.broadcasted_iota(jnp.int32, (own, LANES), 1) % own
    pe_row = jnp.sum(jnp.where(turn, jnp.broadcast_to(pe, (own, LANES)), 0.0), axis=0, keepdims=True)
    pv[me] = jnp.broadcast_to(pe_row, (SUB, LANES))
    ab[r, x] = a_ref[...].T
    expect = len(plane) + jnp.where(z > 0, 1, 0) + jnp.where(z < n_z - 1, 1, 0)
    pl.semaphore_wait(pltpu.get_barrier_semaphore(), expect)

    pending = []

    def piece(b, off):
        if off is None:
            return pb.at[b], n_row * ratio
        row, xx = place(*off)
        return fb.at[row, b, xx], row * ratio + xx

    def hops(s, off):
        def right():
            buf, i = piece(z - s, off)
            return copy(buf, buf, zs.at[0, s, i], zr.at[z - s, i], r, c + ratio)

        def left():
            buf, i = piece(z + s, off)
            return copy(buf, buf, zs.at[1, s, i], zr.at[z + s, i], r, c - ratio)

        return ((z < n_z - 1) & (z >= s), right), ((z > 0) & (z + s < n_z), left)

    def line_send(s, off):
        for go, make in hops(s, off):
            @pl.when(go)
            def _(make=make):
                make().start()

    def line_step(s, off):
        for there, b, (go, make) in zip(((z >= s), (z + s < n_z)), (z - s, z + s), hops(s, off)):
            @pl.when(there)
            def _(b=b):
                buf, i = piece(b, off)
                arrived(buf, zr.at[b, i])

            if s < n_z - 1:
                @pl.when(go)
                def _(make=make):
                    make().start()

    line_send(0, group8[0])
    for i, off in enumerate(plane):
        row, xx = place(*off)
        cp = copy(fp.at[part_of(row) * ratio + xx], fb.at[r, z, x], f1s.at[i], f1r.at[me], row, z * ratio + xx)
        cp.start()
        pending.append(cp)
    for i, off in enumerate(plane):
        row, xx = place(*off)
        cp = copy(pv.at[me], pv.at[me], pvs.at[i], pvr.at[me], row, z * ratio + xx)
        cp.start()
        pending.append(cp)

    def gather_start(buf, at, send, recv, mate_send, mate_recv):
        for i, (dh, dx) in enumerate(peers):
            row, xx = place(dh, dx, 0)
            cp = copy(buf.at[r, x, at], buf.at[r, x, at], send.at[at, i], recv.at[at, h, x], row, z * ratio + xx)
            cp.start()
            pending.append(cp)
        cp = copy(
            buf.at[r, x, at], buf.at[r, x, at], mate_send.at[at, len(peers)], mate_recv.at[at, h, x], mate, c
        )
        cp.start()
        pending.append(cp)

    def gather_relay(buf, at, recv, mate_send, mate_recv):
        for i, (dh, dx) in enumerate(peers):
            row, xx = place(dh, dx, 0)
            hh = row // 2
            arrived(buf.at[row, xx, at], recv.at[at, hh, xx])
            cp = copy(buf.at[row, xx, at], buf.at[row, xx, at], mate_send.at[at, i], mate_recv.at[at, hh, xx], mate, c)
            cp.start()
            pending.append(cp)

    def gather_end(buf, at, mate_recv):
        for hh in range(n_h):
            for xx in range(ratio):
                arrived(buf.at[hh * 2 + 1 - k, xx, at], mate_recv.at[at, hh, xx])

    for i, (dh, dx) in enumerate(peers):
        row, xx = place(dh, dx, 0)
        cp = copy(ab.at[r, x], ab.at[r, x], as_.at[i], ar.at[h, x], row, z * ratio + xx)
        cp.start()
        pending.append(cp)
    cp = copy(ab.at[r, x], ab.at[r, x], ps.at[len(peers)], pr.at[h, x], mate, c)
    cp.start()
    pending.append(cp)
    for off in plane:
        row, xx = place(*off)
        arrived(fb.at[row, z, xx], f1r.at[row * ratio + xx])
        line_send(0, off)
    sub = lax.broadcasted_iota(jnp.int32, (SUB, LANES), 0)
    marks = jnp.where(sub == me, pv[me], 0.0)
    for off in plane:
        row, xx = place(*off)
        i = row * ratio + xx
        arrived(pv.at[i], pvr.at[i])
        marks = jnp.where(sub == i, pv[i], marks)
    pb[z] = marks
    for off in group8:
        line_step(1, off)
    def relay_tiles():
        for i, (dh, dx) in enumerate(peers):
            row, xx = place(dh, dx, 0)
            hh = row // 2
            arrived(ab.at[row, xx], ar.at[hh, xx])
            cp = copy(ab.at[row, xx], ab.at[row, xx], ps.at[i], pr.at[hh, xx], mate, c)
            cp.start()
            pending.append(cp)

    line_send(0, None)
    for s in range(2, n_z):
        for off in group8:
            line_step(s, off)
        if s == 2:
            line_step(1, None)
            relay_tiles()
    for s in range(2, n_z):
        line_step(s, None)
    for hh in range(n_h):
        for xx in range(ratio):
            arrived(ab.at[hh * 2 + 1 - k, xx], pr.at[hh, xx])
    for rr in range(n_row):
        for b in range(n_z):
            for xx in range(ratio):
                top = (b * ratio + xx) * own
                ph, plo = halves(fb[rr, b, xx])
                for ref, val in ((fh, ph), (fl, plo)):
                    ref[rr, top:top + own, :LANES] = val[:own]
                    ref[rr, top:top + half, LANES:] = val[own:, :rest]
                    ref[rr, top + half:top + own, LANES:] = val[own:, rest:]

    def fac(rr):
        return fh[rr], fl[rr]

    for xx in range(ratio):
        m = fh[z, xx * cols:(xx + 1) * cols].astype(jnp.float32)
        m = 0.5 * (m + fl[z, xx * cols:(xx + 1) * cols].astype(jnp.float32))
        for rr in range(n_row):
            m = m + dot3(halves(ab[rr, xx]), fac(rr), NN)
        mx[xx] = m
    left_side = [[v for v in halves(mx[xx])] for xx in range(ratio)]
    left_all = tuple(jnp.concatenate([left_side[xx][i] for xx in range(ratio)], axis=0) for i in range(2))

    order = [n_h - 1 - j for j in range(n_h)]
    for dh in order:
        row = ((h + dh) % n_h) * 2 + 1 - k
        hh = row // 2
        both = dot3(fac(row), left_all, NT)
        for xx in range(ratio):
            sp[row, xx] = both[:, xx * cols:(xx + 1) * cols]
            cp = copy(sp.at[row, xx], sr1.at[hh, xx], s1s.at[hh, xx], s1r.at[hh, xx], mate, c)
            cp.start()
            pending.append(cp)
    for dh in order:
        row = ((h + dh) % n_h) * 2 + k
        both = dot3(fac(row), left_all, NT)
        for xx in range(ratio):
            sp[row, xx] = both[:, xx * cols:(xx + 1) * cols]
    for i, (dh, dx) in enumerate(reversed(peers)):
        row, xx = place(dh, dx, 0)
        hh = row // 2
        arrived(sr1.at[hh, xx], s1r.at[hh, xx])
        sp2[hh, xx] = sp[row, xx] + sr1[hh, xx]
        cp = copy(sp2.at[hh, xx], sr2.at[h, x], s2s.at[i], s2r.at[h, x], row, z * ratio + xx)
        cp.start()
        pending.append(cp)
    arrived(sr1.at[h, x], s1r.at[h, x])
    total = sp[r, x] + sr1[h, x]
    for dh, dx in peers:
        row, xx = place(dh, dx, 0)
        hh = row // 2
        arrived(sr2.at[hh, xx], s2r.at[hh, xx])
        total = total + sr2[hh, xx]
    st[...] = total
    def swap(xx):
        return copy(st.at[pl.ds(xx * cols, cols)], xr.at[x], xs.at[xx], xrs.at[x], z, r * ratio + xx)

    for xx in range(ratio):
        @pl.when((r != z) | (x != xx))
        def _(xx=xx):
            swap(xx).start()

    @pl.when(r == z)
    def _():
        xr[x] = st[pl.ds(pl.multiple_of(x * cols, cols), cols)]

    lane = lax.broadcasted_iota(jnp.int32, (1, LANES), 1)
    group = LANES // own

    def energy(rr, first):
        out = jnp.zeros((1, LANES), jnp.float32)
        for j in range(group):
            at = first + j
            row = pb[at // ratio, pl.ds(rr * ratio + at % ratio, 1)]
            out = jnp.where(lane // own == j, row, out)
        return jnp.broadcast_to(out, (LANES, LANES))

    col_energy = energy(z, x * group)
    row_energy = [energy(r, xx * group).T for xx in range(ratio)]

    for xx in range(ratio):
        @pl.when((r != z) | (x != xx))
        def _(xx=xx):
            arrived(xr.at[xx], xrs.at[xx])

        part = slice(xx * cols, (xx + 1) * cols)
        new = -(st[part] + xr[xx].T) / (row_energy[xx] + col_energy)
        tb[r, x, xx] = new.T
        gather_start(tb, xx, ts, tr, us, ur)
        t_ref[part] = new

    for xx in range(ratio):
        gather_relay(tb, xx, tr, us, ur)
    for xx in range(ratio):
        gather_end(tb, xx, ur)

    def home(xx):
        part = pl.ds(xx * cols, cols)
        return copy(db.at[:, part], o_ref.at[:, part], ds_.at[xx], dr.at[xx], z, goal * ratio + x)

    for xx in range(ratio):
        d = None
        for rr in range(n_row):
            tile = jnp.concatenate([tb[rr, xx, i] for i in range(ratio)], axis=1)
            term = dot3(halves(tile), fac(rr), NN)
            d = term if d is None else d + term
        part = slice(xx * cols, (xx + 1) * cols)
        db[:LANES, part] = d[:, :LANES].T
        db[LANES:, part] = d[:, LANES:].T

        @pl.when(~stays)
        def _(xx=xx):
            home(xx).start()

    @pl.when(stays)
    def _():
        o_ref[...] = db[...]

    for cp in pending:
        cp.wait_send()
    for s in range(n_z - 1):
        for off in group8 + [None]:
            for go, make in hops(s, off):
                @pl.when(go)
                def _(make=make):
                    make().wait_send()
    for xx in range(ratio):
        @pl.when((r != z) | (x != xx))
        def _(xx=xx):
            swap(xx).wait_send()

    @pl.when(~stays)
    def _():
        for xx in range(ratio):
            home(xx).wait_send()
            home(xx).wait_recv()


def settle(new_ref, turned_ref, new_out, turned_out):
    new_out[...] = new_ref[...]
    turned_out[...] = turned_ref[...]


def fits(mesh, rows, cols, own, width):
    n_row, n_col = mesh.shape["row"], mesh.shape["col"]
    ratio = n_col // n_row
    return (
        n_col == ratio * n_row and n_col == SUB and ratio == 2 and n_row % 2 == 0
        and rows == ratio * cols and cols == LANES
        and rows == n_col * own and LANES % own == 0 and own % (4 * SUB) == 0
        and 2 * width == 3 * LANES and 60 * rows * rows * n_row <= 64 * 2**20
    )


def fused(n_row, ratio, amplitudes, factors, occ_map, vir_map, occ_energy, vir_energy):
    rows, cols = amplitudes.shape
    own, n_aux = factors.shape
    n_col = n_row * ratio
    width = n_aux // n_col
    n_h = n_row // 2
    peers = n_h * ratio - 1
    deep = own + own // 2
    f32, bf16 = jnp.float32, jnp.bfloat16
    dma = pltpu.SemaphoreType.DMA
    vmem = pl.BlockSpec(memory_space=pltpu.VMEM)
    new, turned = pl.pallas_call(
        functools.partial(kernel, n_row, ratio, own, width),
        out_shape=(
            jax.ShapeDtypeStruct((rows, cols), f32),
            jax.ShapeDtypeStruct((width, rows), f32),
        ),
        in_specs=[vmem] * 6,
        out_specs=(vmem, vmem),
        scratch_shapes=[
            pltpu.VMEM((n_col, deep, LANES), f32),
            pltpu.VMEM((n_col, SUB, LANES), f32),
            pltpu.VMEM((n_row, SUB, LANES), f32),
            pltpu.VMEM((n_row, n_row, ratio, deep, LANES), f32),
            pltpu.VMEM((n_row, rows, width), bf16),
            pltpu.VMEM((n_row, rows, width), bf16),
            pltpu.VMEM((n_row, ratio, cols, rows), f32),
            pltpu.VMEM((n_row, ratio, rows, cols), f32),
            pltpu.VMEM((n_h, ratio, rows, cols), f32),
            pltpu.VMEM((n_h, ratio, rows, cols), f32),
            pltpu.VMEM((n_h, ratio, rows, cols), f32),
            pltpu.VMEM((rows, cols), f32),
            pltpu.VMEM((ratio, cols, cols), f32),
            pltpu.VMEM((n_row, ratio, ratio, cols, cols), f32),
            pltpu.VMEM((ratio, cols, width), f32),
            pltpu.VMEM((width, rows), f32),
            dma((n_col - 1,)), dma((n_col,)),
            dma((n_col - 1,)), dma((n_col,)),
            dma((2, n_row, n_col + 1)), dma((n_row, n_col + 1)),
            dma((peers,)), dma((n_h, ratio)),
            dma((peers + 1,)), dma((n_h, ratio)),
            dma((n_h, ratio)), dma((n_h, ratio)),
            dma((peers,)), dma((n_h, ratio)),
            dma((ratio,)), dma((ratio,)),
            dma((ratio, peers)), dma((ratio, n_h, ratio)),
            dma((ratio, peers + 1)), dma((ratio, n_h, ratio)),
            dma((ratio,)), dma((ratio,)),
        ],
        compiler_params=pltpu.CompilerParams(collective_id=0, has_side_effects=True),
    )(
        factors, amplitudes, occ_map[None, :], vir_map[None, :], occ_energy[None, :], vir_energy[None, :]
    )
    new, turned = pl.pallas_call(
        settle,
        out_shape=(
            jax.ShapeDtypeStruct((rows, cols), f32),
            jax.ShapeDtypeStruct((width, rows), f32),
        ),
        in_specs=[vmem, vmem],
        out_specs=(vmem, vmem),
    )(new, turned)
    return new, turned.T


def solution(mesh):
    n_row, n_col = mesh.shape["row"], mesh.shape["col"]

    def per_device(amplitudes, factors, *rest):
        rows, cols = amplitudes.shape
        own, n_aux = factors.shape
        if fits(mesh, rows, cols, own, n_aux // n_col):
            return fused(n_row, n_col // n_row, amplitudes, factors, *rest)
        return general(amplitudes, factors, *rest)

    placed = (
        P("row", "col"),
        P(("row", "col"), None),
        P(("row", "col")),
        P(("row", "col")),
        P(),
        P(),
    )
    return jax.shard_map(
        per_device,
        mesh=mesh,
        in_specs=placed,
        out_specs=(P("row", "col"), P("row", "col")),
        check_vma=False,
    )
```

```python
import functools

import jax
import jax.numpy as jnp
from jax import lax
from jax.experimental import pallas as pl
from jax.experimental.pallas import tpu as pltpu
from jax.sharding import PartitionSpec as P

HIGHEST = lax.Precision.HIGHEST
MESH = pl.DeviceIdType.MESH
LANES = 128
SUB = 8


def spread(x, axis, root):
    mine = lax.axis_index(axis) == root
    return lax.psum(jnp.where(mine, x, jnp.zeros_like(x)), axis)


def pair_energies(occ_map, vir_map, occ_energy, vir_energy):
    def pick(index, table):
        hot = index[:, None] == jnp.arange(table.shape[0], dtype=jnp.int32)[None, :]
        return jnp.sum(jnp.where(hot, table[None, :], 0.0), axis=1)

    return pick(vir_map, vir_energy) - pick(occ_map, occ_energy)


def general(amplitudes, factors, occ_map, vir_map, occ_energy, vir_energy):
    col_ratio = lax.axis_size("col") // lax.axis_size("row")
    column = lax.axis_index("col")
    pair_energy = pair_energies(occ_map, vir_map, occ_energy, vir_energy)
    row_factor, row_energy = (
        lax.all_gather(factors, "col", axis=0, tiled=True),
        lax.all_gather(pair_energy, "col", axis=0, tiled=True),
    )
    tile_width = amplitudes.shape[1]
    offset = column % col_ratio * tile_width
    source = column // col_ratio
    col_factor, col_energy = (
        spread(lax.dynamic_slice_in_dim(row_factor, offset, tile_width, 0), "row", source),
        spread(lax.dynamic_slice_in_dim(row_energy, offset, tile_width, 0), "row", source),
    )
    mixed_rows = lax.psum(
        jnp.dot(amplitudes, col_factor, precision=HIGHEST, preferred_element_type=jnp.float32),
        "col",
    )
    transposed = lax.dot_general(
        amplitudes,
        row_factor,
        (((0,), (0,)), ((), ())),
        precision=HIGHEST,
        preferred_element_type=jnp.float32,
    )
    mixed_cols = lax.psum(transposed, "row")
    contract = (((1,), (1,)), ((), ()))
    residual = lax.dot_general(
        row_factor + mixed_rows,
        col_factor,
        contract,
        precision=HIGHEST,
        preferred_element_type=jnp.float32,
    )
    residual = residual + lax.dot_general(
        row_factor, mixed_cols, contract, precision=HIGHEST, preferred_element_type=jnp.float32
    )
    new_amp = -residual / (row_energy[:, None] + col_energy[None, :])
    dens_terms = jnp.dot(new_amp, col_factor, precision=HIGHEST, preferred_element_type=jnp.float32)
    density = lax.psum_scatter(dens_terms, "col", scatter_dimension=1, tiled=True)
    return (new_amp, density)


def halves(v):
    high = v.astype(jnp.bfloat16)
    return high, (v - high.astype(jnp.float32)).astype(jnp.bfloat16)


def dot3(a, b, dims):
    (ah, al), (bh, bl) = a, b
    dot = functools.partial(
        lax.dot_general, dimension_numbers=(dims, ((), ())), preferred_element_type=jnp.float32
    )
    return dot(ah, bh) + (dot(ah, bl) + dot(al, bh))


NN = ((1,), (0,))
NT = ((1,), (1,))


def kernel(
    n_row, ratio, own, width,
    f_hbm, a_hbm, om_hbm, vm_hbm, oe_hbm, ve_hbm, t_ref, o_ref,
    f_ref, a_ref, om_ref, vm_ref, oe_ref, ve_ref,
    fp, pv, pb, fb, fh, fl, ab, sp, so, sr, ax, axr, ay, ayr, bx, bxr, by, byr, st, xr, tb, mx, db,
    ld, f1s, f1r, pvs, pvr, zs, zr, as_, ar, ps, pr, ms, mr, rs, rr_, xs, xrs,
    ts, tr, us, ur, ds_, dr,
):
    n_z = n_row
    r = lax.axis_index("row")
    c = lax.axis_index("col")
    z, x = c // ratio, c % ratio
    k = r % 2
    h = r // 2
    mate = r + 1 - 2 * k
    near_x = (r, z * ratio + 1 - x)
    near_y = ((1 - r // 2) * 2 + k, c)
    n_h = n_row // 2
    rows, cols = a_ref.shape
    fine = cols // 2
    half = own // 2
    rest = width - LANES
    me = r * ratio + x

    def part_of(row):
        return (row % 2) * n_h + row // 2

    goal = part_of(r)
    stays = (r == z) & (goal == z)

    def copy(src, dst, send, recv, row, col):
        return pltpu.make_async_remote_copy(
            src_ref=src, dst_ref=dst, send_sem=send, recv_sem=recv,
            device_id=(row, col), device_id_type=MESH,
        )

    def arrived(buf, recv):
        copy(buf, buf, ds_.at[0], recv, mate, c).wait_recv()

    def greet(row, col):
        pl.semaphore_signal(
            pltpu.get_barrier_semaphore(), inc=1, device_id=(row, col), device_id_type=MESH
        )

    def place(dh, dx, dk):
        return ((h + dh) % n_h) * 2 + (k + dk) % 2, (x + dx) % ratio

    group8 = [(dh, dx, dk) for dh in range(n_h) for dx in range(ratio) for dk in range(2)]
    plane = group8[1:]
    peers = [(dh, dx) for dh in range(n_h) for dx in range(ratio) if dh or dx]

    for off in plane:
        row, xx = place(*off)
        greet(row, z * ratio + xx)

    @pl.when(z > 0)
    def _():
        greet(r, c - ratio)

    @pl.when(z < n_z - 1)
    def _():
        greet(r, c + ratio)

    loads = [
        pltpu.make_async_copy(src, dst, ld.at[i])
        for i, (src, dst) in enumerate((
            (f_hbm, f_ref), (a_hbm, a_ref), (om_hbm, om_ref), (vm_hbm, vm_ref), (oe_hbm, oe_ref), (ve_hbm, ve_ref)
        ))
    ]
    for load in loads:
        load.start()
    loads[0].wait()
    for p in range(n_row * ratio):
        fp[p, :own] = f_ref[:, p * width:p * width + LANES]
        tail = f_ref[:, p * width + LANES:(p + 1) * width]
        fp[p, own:] = jnp.concatenate([tail[:half], tail[half:]], axis=1)
    fb[r, z, x] = fp[goal * ratio + x]

    def pick(index_ref, table_ref):
        size = table_ref.shape[1]
        index = jnp.broadcast_to(index_ref[...].astype(jnp.float32), (own, own))
        diag = lax.broadcasted_iota(jnp.int32, (own, own), 0) == lax.broadcasted_iota(jnp.int32, (own, own), 1)
        column = jnp.sum(jnp.where(diag, index, 0.0), axis=1, keepdims=True)
        spot = lax.broadcasted_iota(jnp.int32, (own, size), 1).astype(jnp.float32)
        table = jnp.broadcast_to(table_ref[...], (own, size))
        return jnp.sum(jnp.where(spot == column, table, 0.0), axis=1, keepdims=True)

    for load in loads[1:]:
        load.wait()
    pe = pick(vm_ref, ve_ref) - pick(om_ref, oe_ref)
    turn = lax.broadcasted_iota(jnp.int32, (own, LANES), 0) == lax.broadcasted_iota(jnp.int32, (own, LANES), 1) % own
    pe_row = jnp.sum(jnp.where(turn, jnp.broadcast_to(pe, (own, LANES)), 0.0), axis=0, keepdims=True)
    pv[me] = jnp.broadcast_to(pe_row, (SUB, LANES))
    ab[r, x] = a_ref[...].T
    expect = len(plane) + jnp.where(z > 0, 1, 0) + jnp.where(z < n_z - 1, 1, 0)
    pl.semaphore_wait(pltpu.get_barrier_semaphore(), expect)

    pending = []

    def piece(b, off):
        if off is None:
            return pb.at[b], n_row * ratio
        row, xx = place(*off)
        return fb.at[row, b, xx], row * ratio + xx

    def hops(s, off):
        def right():
            buf, i = piece(z - s, off)
            return copy(buf, buf, zs.at[0, s, i], zr.at[z - s, i], r, c + ratio)

        def left():
            buf, i = piece(z + s, off)
            return copy(buf, buf, zs.at[1, s, i], zr.at[z + s, i], r, c - ratio)

        return ((z < n_z - 1) & (z >= s), right), ((z > 0) & (z + s < n_z), left)

    def line_send(s, off):
        for go, make in hops(s, off):
            @pl.when(go)
            def _(make=make):
                make().start()

    def line_step(s, off):
        for there, b, (go, make) in zip(((z >= s), (z + s < n_z)), (z - s, z + s), hops(s, off)):
            @pl.when(there)
            def _(b=b):
                buf, i = piece(b, off)
                arrived(buf, zr.at[b, i])

            if s < n_z - 1:
                @pl.when(go)
                def _(make=make):
                    make().start()

    line_send(0, group8[0])
    for i, off in enumerate(plane):
        row, xx = place(*off)
        cp = copy(fp.at[part_of(row) * ratio + xx], fb.at[r, z, x], f1s.at[i], f1r.at[me], row, z * ratio + xx)
        cp.start()
        pending.append(cp)
    for i, off in enumerate(plane):
        row, xx = place(*off)
        cp = copy(pv.at[me], pv.at[me], pvs.at[i], pvr.at[me], row, z * ratio + xx)
        cp.start()
        pending.append(cp)

    def send(src, dst, out, into, row, col):
        cp = copy(src, dst, out, into, row, col)
        cp.start()
        pending.append(cp)

    for i, (dh, dx) in enumerate(peers):
        row, xx = place(dh, dx, 0)
        cp = copy(ab.at[r, x], ab.at[r, x], as_.at[i], ar.at[h, x], row, z * ratio + xx)
        cp.start()
        pending.append(cp)
    cp = copy(ab.at[r, x], ab.at[r, x], ps.at[len(peers)], pr.at[h, x], mate, c)
    cp.start()
    pending.append(cp)
    for off in plane:
        row, xx = place(*off)
        arrived(fb.at[row, z, xx], f1r.at[row * ratio + xx])
        line_send(0, off)
    sub = lax.broadcasted_iota(jnp.int32, (SUB, LANES), 0)
    marks = jnp.where(sub == me, pv[me], 0.0)
    for off in plane:
        row, xx = place(*off)
        i = row * ratio + xx
        arrived(pv.at[i], pvr.at[i])
        marks = jnp.where(sub == i, pv[i], marks)
    pb[z] = marks
    for off in group8:
        line_step(1, off)
    def relay_tiles():
        for i, (dh, dx) in enumerate(peers):
            row, xx = place(dh, dx, 0)
            hh = row // 2
            arrived(ab.at[row, xx], ar.at[hh, xx])
            cp = copy(ab.at[row, xx], ab.at[row, xx], ps.at[i], pr.at[hh, xx], mate, c)
            cp.start()
            pending.append(cp)

    line_send(0, None)
    for s in range(2, n_z):
        for off in group8:
            line_step(s, off)
        if s == 2:
            line_step(1, None)
            relay_tiles()
    for s in range(2, n_z):
        line_step(s, None)
    for hh in range(n_h):
        for xx in range(ratio):
            arrived(ab.at[hh * 2 + 1 - k, xx], pr.at[hh, xx])
    for rr in range(n_row):
        for b in range(n_z):
            for xx in range(ratio):
                top = (b * ratio + xx) * own
                ph, plo = halves(fb[rr, b, xx])
                for ref, val in ((fh, ph), (fl, plo)):
                    ref[rr, top:top + own, :LANES] = val[:own]
                    ref[rr, top:top + half, LANES:] = val[own:, :rest]
                    ref[rr, top + half:top + own, LANES:] = val[own:, rest:]

    def fac(rr):
        return fh[rr], fl[rr]

    for xx in range(ratio):
        m = fh[z, xx * cols:(xx + 1) * cols].astype(jnp.float32)
        m = 0.5 * (m + fl[z, xx * cols:(xx + 1) * cols].astype(jnp.float32))
        for rr in range(n_row):
            m = m + dot3(halves(ab[rr, xx]), fac(rr), NN)
        mx[xx] = m
    left_side = [[v for v in halves(mx[xx])] for xx in range(ratio)]
    left_all = tuple(jnp.concatenate([left_side[xx][i] for xx in range(ratio)], axis=0) for i in range(2))

    def strip(row, q):
        parts = [slice(j * cols + q * fine, j * cols + (q + 1) * fine) for j in range(ratio)]
        return tuple(jnp.concatenate([ref[row, part] for part in parts], axis=0) for ref in (fh, fl))

    def products(ref, q, yy, row):
        both = dot3(strip(row, q), left_all, NT)
        for j in range(ratio):
            for xx in range(ratio):
                ref[q, yy, j, xx] = both[j * fine:(j + 1) * fine, xx * cols:(xx + 1) * cols]

    for q in range(2):
        for yy in range(n_h):
            products(sp, q, yy, yy * 2 + 1 - k)
        send(sp.at[q], sr.at[q], ms.at[q], mr.at[q], mate, c)
    for q in range(2):
        for yy in range(n_h):
            products(so, q, yy, yy * 2 + k)

    def pair(q, yy, j, xx):
        return so[q, yy, j, xx] + sr[q, yy, j, xx]

    for q in range(2):
        arrived(sr.at[q], mr.at[q])
        for yy in range(n_h):
            ax[q, yy] = pair(q, yy, 0, 1 - x)
        send(ax.at[q], axr.at[q], rs.at[q, 0], rr_.at[q, 0], *near_x)
        for xx in range(ratio):
            ay[q, xx] = pair(q, 1 - h, 1, xx)
        send(ay.at[q], ayr.at[q], rs.at[q, 1], rr_.at[q, 1], *near_y)
    for q in range(2):
        arrived(axr.at[q], rr_.at[q, 0])
        bx[q] = pair(q, 1 - h, 0, x) + axr[q, 1 - h]
        send(bx.at[q], bxr.at[q], rs.at[q, 2], rr_.at[q, 2], *near_y)
        arrived(ayr.at[q], rr_.at[q, 1])
        by[q] = pair(q, h, 1, 1 - x) + ayr[q, 1 - x]
        send(by.at[q], byr.at[q], rs.at[q, 3], rr_.at[q, 3], *near_x)

    def swap(q, j):
        return copy(
            st.at[pl.ds(j * cols + q * fine, fine)], xr.at[x, pl.ds(q * fine, fine)],
            xs.at[q, j], xrs.at[q, x], z, r * ratio + j,
        )

    for q in range(2):
        low, high = slice(q * fine, (q + 1) * fine), slice(cols + q * fine, cols + (q + 1) * fine)
        arrived(bxr.at[q], rr_.at[q, 2])
        st[low] = pair(q, h, 0, x) + axr[q, h] + bxr[q]
        arrived(byr.at[q], rr_.at[q, 3])
        st[high] = pair(q, h, 1, x) + ayr[q, x] + byr[q]
        for j in range(ratio):
            @pl.when((r != z) | (x != j))
            def _(q=q, j=j):
                swap(q, j).start()

        @pl.when(r == z)
        def _(q=q, low=low):
            xr[x, low] = st[pl.ds(pl.multiple_of(x * cols + q * fine, fine), fine)]

    lane = lax.broadcasted_iota(jnp.int32, (1, LANES), 1)
    group = LANES // own

    def energy(rr, first):
        out = jnp.zeros((1, LANES), jnp.float32)
        for j in range(group):
            at = first + j
            row = pb[at // ratio, pl.ds(rr * ratio + at % ratio, 1)]
            out = jnp.where(lane // own == j, row, out)
        return jnp.broadcast_to(out, (LANES, LANES))

    col_energy = energy(z, x * group).T
    bottom = [col_energy + energy(r, j * group) for j in range(ratio)]
    top = [st[j * cols:(j + 1) * cols].T for j in range(ratio)]

    def share(q):
        part = slice(q * fine, (q + 1) * fine)
        for xx in range(ratio):
            @pl.when((r != z) | (x != xx))
            def _(xx=xx):
                arrived(xr.at[xx, pl.ds(q * fine, fine)], xrs.at[q, xx])

        for j in range(ratio):
            tb[r, x, j, part] = -(top[j][part] + xr[j, part]) / bottom[j][part]
        for way, near in enumerate((near_x, near_y, (near_y[0], near_x[1]))):
            send(tile(r, x, q), tile(r, x, q), ts.at[q, way], tr.at[q, way], *near)
        relay(r, x, q, 0)

    def tile(row, xx, q):
        return tb.at[row, xx, :, pl.ds(q * fine, fine)]

    def relay(row, xx, q, i):
        send(tile(row, xx, q), tile(row, xx, q), us.at[q, i], ur.at[q, i], mate, c)

    def collect(q):
        for way, (row, xx) in enumerate(((r, 1 - x), (near_y[0], x), (near_y[0], 1 - x))):
            arrived(tile(row, xx, q), tr.at[q, way])
            relay(row, xx, q, 1 + way)

    def finish(q):
        other = near_y[0] + mate - r
        for i, (row, xx) in enumerate(((mate, x), (mate, 1 - x), (other, x), (other, 1 - x))):
            arrived(tile(row, xx, q), ur.at[q, i])

    def home(q):
        return copy(db.at[q], o_ref.at[q], ds_.at[q], dr.at[q], z, goal * ratio + x)

    def density(q):
        d = None
        part = slice(q * fine, (q + 1) * fine)
        for rr in range(n_row):
            block = jnp.concatenate([
                jnp.concatenate([tb[rr, xx, j, part] for j in range(ratio)], axis=1) for xx in range(ratio)
            ], axis=0)
            term = dot3(halves(block), fac(rr), NN)
            d = term if d is None else d + term
        db[q, :LANES] = d[:, :LANES].T
        db[q, LANES:] = d[:, LANES:].T

        @pl.when(~stays)
        def _():
            home(q).start()

        @pl.when(stays)
        def _():
            o_ref[q] = db[q]

    share(0)
    share(1)
    collect(0)
    finish(0)
    density(0)
    collect(1)
    for j in range(ratio):
        t_ref[j * cols:(j + 1) * cols] = tb[r, x, j].T
    finish(1)
    density(1)

    for cp in pending:
        cp.wait_send()
    for s in range(n_z - 1):
        for off in group8 + [None]:
            for go, make in hops(s, off):
                @pl.when(go)
                def _(make=make):
                    make().wait_send()
    for q in range(2):
        for j in range(ratio):
            @pl.when((r != z) | (x != j))
            def _(q=q, j=j):
                swap(q, j).wait_send()

    @pl.when(~stays)
    def _():
        for q in range(2):
            home(q).wait_send()
            home(q).wait_recv()


def settle(new_ref, turned_ref, new_out, turned_out):
    new_out[...] = new_ref[...]
    low, high = turned_ref[0], turned_ref[1]
    half = low.shape[1] // 2
    turned_out[:, :2 * half] = jnp.concatenate([low[:, :half], high[:, :half]], axis=1)
    turned_out[:, 2 * half:] = jnp.concatenate([low[:, half:], high[:, half:]], axis=1)


def fits(mesh, rows, cols, own, width):
    n_row, n_col = mesh.shape["row"], mesh.shape["col"]
    ratio = n_col // n_row
    return (
        n_col == ratio * n_row and n_col == SUB and ratio == 2 and n_row == 4
        and rows == ratio * cols and cols == LANES
        and rows == n_col * own and LANES % own == 0 and own % (4 * SUB) == 0
        and 2 * width == 3 * LANES and 60 * rows * rows * n_row <= 64 * 2**20
    )


def fused(n_row, ratio, amplitudes, factors, occ_map, vir_map, occ_energy, vir_energy):
    rows, cols = amplitudes.shape
    own, n_aux = factors.shape
    n_col = n_row * ratio
    width = n_aux // n_col
    n_h = n_row // 2
    peers = n_h * ratio - 1
    deep = own + own // 2
    f32, bf16 = jnp.float32, jnp.bfloat16
    dma = pltpu.SemaphoreType.DMA
    vmem = pl.BlockSpec(memory_space=pltpu.VMEM)
    fine = cols // 2
    new, turned = pl.pallas_call(
        functools.partial(kernel, n_row, ratio, own, width),
        out_shape=(
            jax.ShapeDtypeStruct((rows, cols), f32),
            jax.ShapeDtypeStruct((2, width, cols), f32),
        ),
        in_specs=[pl.BlockSpec(memory_space=pltpu.HBM)] * 6,
        out_specs=(vmem, vmem),
        scratch_shapes=[
            pltpu.VMEM(factors.shape, f32),
            pltpu.VMEM((rows, cols), f32),
            pltpu.VMEM((1, own), jnp.int32),
            pltpu.VMEM((1, own), jnp.int32),
            pltpu.VMEM((1,) + occ_energy.shape, f32),
            pltpu.VMEM((1,) + vir_energy.shape, f32),
            pltpu.VMEM((n_col, deep, LANES), f32),
            pltpu.VMEM((n_col, SUB, LANES), f32),
            pltpu.VMEM((n_row, SUB, LANES), f32),
            pltpu.VMEM((n_row, n_row, ratio, deep, LANES), f32),
            pltpu.VMEM((n_row, rows, width), bf16),
            pltpu.VMEM((n_row, rows, width), bf16),
            pltpu.VMEM((n_row, ratio, cols, rows), f32),
            pltpu.VMEM((2, n_h, ratio, ratio, fine, cols), f32),
            pltpu.VMEM((2, n_h, ratio, ratio, fine, cols), f32),
            pltpu.VMEM((2, n_h, ratio, ratio, fine, cols), f32),
            pltpu.VMEM((2, n_h, fine, cols), f32),
            pltpu.VMEM((2, n_h, fine, cols), f32),
            pltpu.VMEM((2, ratio, fine, cols), f32),
            pltpu.VMEM((2, ratio, fine, cols), f32),
            pltpu.VMEM((2, fine, cols), f32),
            pltpu.VMEM((2, fine, cols), f32),
            pltpu.VMEM((2, fine, cols), f32),
            pltpu.VMEM((2, fine, cols), f32),
            pltpu.VMEM((rows, cols), f32),
            pltpu.VMEM((ratio, cols, cols), f32),
            pltpu.VMEM((n_row, ratio, ratio, cols, cols), f32),
            pltpu.VMEM((ratio, cols, width), f32),
            pltpu.VMEM((2, width, cols), f32),
            dma((6,)),
            dma((n_col - 1,)), dma((n_col,)),
            dma((n_col - 1,)), dma((n_col,)),
            dma((2, n_row, n_col + 1)), dma((n_row, n_col + 1)),
            dma((peers,)), dma((n_h, ratio)),
            dma((peers + 1,)), dma((n_h, ratio)),
            dma((2,)), dma((2,)),
            dma((2, 4)), dma((2, 4)),
            dma((2, ratio)), dma((2, ratio)),
            dma((2, 3)), dma((2, 3)),
            dma((2, 4)), dma((2, 4)),
            dma((2,)), dma((2,)),
        ],
        compiler_params=pltpu.CompilerParams(
            collective_id=0, has_side_effects=True
        ),
    )(
        factors, amplitudes, occ_map[None, :], vir_map[None, :], occ_energy[None, :], vir_energy[None, :]
    )
    new, turned = pl.pallas_call(
        settle,
        out_shape=(
            jax.ShapeDtypeStruct((rows, cols), f32),
            jax.ShapeDtypeStruct((width, rows), f32),
        ),
        in_specs=[vmem, vmem],
        out_specs=(vmem, vmem),
    )(new, turned)
    return new, turned.T


def solution(mesh):
    n_row, n_col = mesh.shape["row"], mesh.shape["col"]

    def per_device(amplitudes, factors, *rest):
        rows, cols = amplitudes.shape
        own, n_aux = factors.shape
        if fits(mesh, rows, cols, own, n_aux // n_col):
            return fused(n_row, n_col // n_row, amplitudes, factors, *rest)
        return general(amplitudes, factors, *rest)

    placed = (
        P("row", "col"),
        P(("row", "col"), None),
        P(("row", "col")),
        P(("row", "col")),
        P(),
        P(),
    )
    return jax.shard_map(
        per_device,
        mesh=mesh,
        in_specs=placed,
        out_specs=(P("row", "col"), P("row", "col")),
        check_vma=False,
    )
```

```python
import functools

import jax
import jax.numpy as jnp
from jax import lax
from jax.experimental import pallas as pl
from jax.experimental.pallas import tpu as pltpu
from jax.sharding import PartitionSpec as P

HIGHEST = lax.Precision.HIGHEST
MESH = pl.DeviceIdType.MESH
LANES = 128
SUB = 8


def spread(x, axis, root):
    mine = lax.axis_index(axis) == root
    return lax.psum(jnp.where(mine, x, jnp.zeros_like(x)), axis)


def pair_energies(occ_map, vir_map, occ_energy, vir_energy):
    def pick(index, table):
        hot = index[:, None] == jnp.arange(table.shape[0], dtype=jnp.int32)[None, :]
        return jnp.sum(jnp.where(hot, table[None, :], 0.0), axis=1)

    return pick(vir_map, vir_energy) - pick(occ_map, occ_energy)


def general(amplitudes, factors, occ_map, vir_map, occ_energy, vir_energy):
    col_ratio = lax.axis_size("col") // lax.axis_size("row")
    column = lax.axis_index("col")
    pair_energy = pair_energies(occ_map, vir_map, occ_energy, vir_energy)
    row_factor, row_energy = (
        lax.all_gather(factors, "col", axis=0, tiled=True),
        lax.all_gather(pair_energy, "col", axis=0, tiled=True),
    )
    tile_width = amplitudes.shape[1]
    offset = column % col_ratio * tile_width
    source = column // col_ratio
    col_factor, col_energy = (
        spread(lax.dynamic_slice_in_dim(row_factor, offset, tile_width, 0), "row", source),
        spread(lax.dynamic_slice_in_dim(row_energy, offset, tile_width, 0), "row", source),
    )
    mixed_rows = lax.psum(
        jnp.dot(amplitudes, col_factor, precision=HIGHEST, preferred_element_type=jnp.float32),
        "col",
    )
    transposed = lax.dot_general(
        amplitudes,
        row_factor,
        (((0,), (0,)), ((), ())),
        precision=HIGHEST,
        preferred_element_type=jnp.float32,
    )
    mixed_cols = lax.psum(transposed, "row")
    contract = (((1,), (1,)), ((), ()))
    residual = lax.dot_general(
        row_factor + mixed_rows,
        col_factor,
        contract,
        precision=HIGHEST,
        preferred_element_type=jnp.float32,
    )
    residual = residual + lax.dot_general(
        row_factor, mixed_cols, contract, precision=HIGHEST, preferred_element_type=jnp.float32
    )
    new_amp = -residual / (row_energy[:, None] + col_energy[None, :])
    dens_terms = jnp.dot(new_amp, col_factor, precision=HIGHEST, preferred_element_type=jnp.float32)
    density = lax.psum_scatter(dens_terms, "col", scatter_dimension=1, tiled=True)
    return (new_amp, density)


def halves(v):
    high = v.astype(jnp.bfloat16)
    return high, (v - high.astype(jnp.float32)).astype(jnp.bfloat16)


def dot3(a, b, dims):
    (ah, al), (bh, bl) = a, b
    dot = functools.partial(
        lax.dot_general, dimension_numbers=(dims, ((), ())), preferred_element_type=jnp.float32
    )
    return dot(ah, bh) + (dot(ah, bl) + dot(al, bh))


NN = ((1,), (0,))
NT = ((1,), (1,))


def kernel(
    n_row, ratio, own, width,
    f_hbm, a_hbm, om_hbm, vm_hbm, oe_hbm, ve_hbm, t_ref, o_ref,
    f_ref, a_ref, om_ref, vm_ref, oe_ref, ve_ref,
    fp, pv, pb, fb, fh, fl, ab, sp, so, sr, ax, axr, ay, ayr, bx, bxr, by, byr, st, xr, tb, mx, db,
    ld, f1s, f1r, pvs, pvr, zs, zr, as_, ar, ps, pr, ms, mr, rs, rr_, xs, xrs,
    ts, tr, us, ur, ds_, dr,
):
    n_z = n_row
    r = lax.axis_index("row")
    c = lax.axis_index("col")
    z, x = c // ratio, c % ratio
    k = r % 2
    h = r // 2
    mate = r + 1 - 2 * k
    near_x = (r, z * ratio + 1 - x)
    near_y = ((1 - r // 2) * 2 + k, c)
    n_h = n_row // 2
    rows, cols = a_ref.shape
    fine = cols // 2
    half = own // 2
    rest = width - LANES
    me = r * ratio + x

    def part_of(row):
        return (row % 2) * n_h + row // 2

    goal = part_of(r)
    stays = (r == z) & (goal == z)

    def copy(src, dst, send, recv, row, col):
        return pltpu.make_async_remote_copy(
            src_ref=src, dst_ref=dst, send_sem=send, recv_sem=recv,
            device_id=(row, col), device_id_type=MESH,
        )

    def arrived(buf, recv):
        copy(buf, buf, ds_.at[0], recv, mate, c).wait_recv()

    def greet(row, col):
        pl.semaphore_signal(
            pltpu.get_barrier_semaphore(), inc=1, device_id=(row, col), device_id_type=MESH
        )

    def place(dh, dx, dk):
        return ((h + dh) % n_h) * 2 + (k + dk) % 2, (x + dx) % ratio

    group8 = [(dh, dx, dk) for dh in range(n_h) for dx in range(ratio) for dk in range(2)]
    plane = group8[1:]
    peers = [(dh, dx) for dh in range(n_h) for dx in range(ratio) if dh or dx]

    for off in plane:
        row, xx = place(*off)
        greet(row, z * ratio + xx)

    @pl.when(z > 0)
    def _():
        greet(r, c - ratio)

    @pl.when(z < n_z - 1)
    def _():
        greet(r, c + ratio)

    loads = [
        pltpu.make_async_copy(src, dst, ld.at[i])
        for i, (src, dst) in enumerate((
            (f_hbm, f_ref), (a_hbm, a_ref), (om_hbm, om_ref), (vm_hbm, vm_ref), (oe_hbm, oe_ref), (ve_hbm, ve_ref)
        ))
    ]
    for load in loads:
        load.start()
    loads[0].wait()
    for p in range(n_row * ratio):
        fp[p, :own] = f_ref[:, p * width:p * width + LANES]
        tail = f_ref[:, p * width + LANES:(p + 1) * width]
        fp[p, own:] = jnp.concatenate([tail[:half], tail[half:]], axis=1)
    fb[r, z, x] = fp[goal * ratio + x]

    def pick(index_ref, table_ref):
        size = table_ref.shape[1]
        index = jnp.broadcast_to(index_ref[...].astype(jnp.float32), (own, own))
        diag = lax.broadcasted_iota(jnp.int32, (own, own), 0) == lax.broadcasted_iota(jnp.int32, (own, own), 1)
        column = jnp.sum(jnp.where(diag, index, 0.0), axis=1, keepdims=True)
        spot = lax.broadcasted_iota(jnp.int32, (own, size), 1).astype(jnp.float32)
        table = jnp.broadcast_to(table_ref[...], (own, size))
        return jnp.sum(jnp.where(spot == column, table, 0.0), axis=1, keepdims=True)

    for load in loads[1:]:
        load.wait()
    pe = pick(vm_ref, ve_ref) - pick(om_ref, oe_ref)
    turn = lax.broadcasted_iota(jnp.int32, (own, LANES), 0) == lax.broadcasted_iota(jnp.int32, (own, LANES), 1) % own
    pe_row = jnp.sum(jnp.where(turn, jnp.broadcast_to(pe, (own, LANES)), 0.0), axis=0, keepdims=True)
    pv[me] = jnp.broadcast_to(pe_row, (SUB, LANES))
    ab[r, x] = a_ref[...].T
    expect = len(plane) + jnp.where(z > 0, 1, 0) + jnp.where(z < n_z - 1, 1, 0)
    pl.semaphore_wait(pltpu.get_barrier_semaphore(), expect)

    pending = []

    def piece(b, off):
        if off is None:
            return pb.at[b], n_row * ratio
        row, xx = place(*off)
        return fb.at[row, b, xx], row * ratio + xx

    def hops(s, off):
        def right():
            buf, i = piece(z - s, off)
            return copy(buf, buf, zs.at[0, s, i], zr.at[z - s, i], r, c + ratio)

        def left():
            buf, i = piece(z + s, off)
            return copy(buf, buf, zs.at[1, s, i], zr.at[z + s, i], r, c - ratio)

        return ((z < n_z - 1) & (z >= s), right), ((z > 0) & (z + s < n_z), left)

    def line_send(s, off):
        for go, make in hops(s, off):
            @pl.when(go)
            def _(make=make):
                make().start()

    def line_step(s, off):
        for there, b, (go, make) in zip(((z >= s), (z + s < n_z)), (z - s, z + s), hops(s, off)):
            @pl.when(there)
            def _(b=b):
                buf, i = piece(b, off)
                arrived(buf, zr.at[b, i])

            if s < n_z - 1:
                @pl.when(go)
                def _(make=make):
                    make().start()

    line_send(0, group8[0])
    for i, off in enumerate(plane):
        row, xx = place(*off)
        cp = copy(fp.at[part_of(row) * ratio + xx], fb.at[r, z, x], f1s.at[i], f1r.at[me], row, z * ratio + xx)
        cp.start()
        pending.append(cp)
    for i, off in enumerate(plane):
        row, xx = place(*off)
        cp = copy(pv.at[me], pv.at[me], pvs.at[i], pvr.at[me], row, z * ratio + xx)
        cp.start()
        pending.append(cp)

    def send(src, dst, out, into, row, col):
        cp = copy(src, dst, out, into, row, col)
        cp.start()
        pending.append(cp)

    for i, (dh, dx) in enumerate(peers):
        row, xx = place(dh, dx, 0)
        cp = copy(ab.at[r, x], ab.at[r, x], as_.at[i], ar.at[h, x], row, z * ratio + xx)
        cp.start()
        pending.append(cp)
    cp = copy(ab.at[r, x], ab.at[r, x], ps.at[len(peers)], pr.at[h, x], mate, c)
    cp.start()
    pending.append(cp)
    for off in plane:
        row, xx = place(*off)
        arrived(fb.at[row, z, xx], f1r.at[row * ratio + xx])
        line_send(0, off)
    sub = lax.broadcasted_iota(jnp.int32, (SUB, LANES), 0)
    marks = jnp.where(sub == me, pv[me], 0.0)
    for off in plane:
        row, xx = place(*off)
        i = row * ratio + xx
        arrived(pv.at[i], pvr.at[i])
        marks = jnp.where(sub == i, pv[i], marks)
    pb[z] = marks
    for off in group8:
        line_step(1, off)
    def relay_tiles():
        for i, (dh, dx) in enumerate(peers):
            row, xx = place(dh, dx, 0)
            hh = row // 2
            arrived(ab.at[row, xx], ar.at[hh, xx])
            cp = copy(ab.at[row, xx], ab.at[row, xx], ps.at[i], pr.at[hh, xx], mate, c)
            cp.start()
            pending.append(cp)

    line_send(0, None)
    for s in range(2, n_z):
        for off in group8:
            line_step(s, off)
        if s == 2:
            line_step(1, None)
            relay_tiles()
    for s in range(2, n_z):
        line_step(s, None)
    for hh in range(n_h):
        for xx in range(ratio):
            arrived(ab.at[hh * 2 + 1 - k, xx], pr.at[hh, xx])
    for rr in range(n_row):
        for b in range(n_z):
            for xx in range(ratio):
                top = (b * ratio + xx) * own
                ph, plo = halves(fb[rr, b, xx])
                for ref, val in ((fh, ph), (fl, plo)):
                    ref[rr, top:top + own, :LANES] = val[:own]
                    ref[rr, top:top + half, LANES:] = val[own:, :rest]
                    ref[rr, top + half:top + own, LANES:] = val[own:, rest:]

    def fac(rr):
        return fh[rr], fl[rr]

    for xx in range(ratio):
        m = fh[z, xx * cols:(xx + 1) * cols].astype(jnp.float32)
        m = 0.5 * (m + fl[z, xx * cols:(xx + 1) * cols].astype(jnp.float32))
        for rr in range(n_row):
            m = m + dot3(halves(ab[rr, xx]), fac(rr), NN)
        mx[xx] = m
    left_side = [[v for v in halves(mx[xx])] for xx in range(ratio)]
    left_all = tuple(jnp.concatenate([left_side[xx][i] for xx in range(ratio)], axis=0) for i in range(2))

    def strip(row, q):
        parts = [slice(j * cols + q * fine, j * cols + (q + 1) * fine) for j in range(ratio)]
        return tuple(jnp.concatenate([ref[row, part] for part in parts], axis=0) for ref in (fh, fl))

    def products(ref, q, yy, row):
        both = dot3(strip(row, q), left_all, NT)
        for j in range(ratio):
            for xx in range(ratio):
                ref[q, yy, j, xx] = both[j * fine:(j + 1) * fine, xx * cols:(xx + 1) * cols]

    for q in range(2):
        for yy in range(n_h):
            products(sp, q, yy, yy * 2 + 1 - k)
        send(sp.at[q], sr.at[q], ms.at[q], mr.at[q], mate, c)
    for q in range(2):
        for yy in range(n_h):
            products(so, q, yy, yy * 2 + k)

    def pair(q, yy, j, xx):
        return so[q, yy, j, xx] + sr[q, yy, j, xx]

    for q in range(2):
        arrived(sr.at[q], mr.at[q])
        for yy in range(n_h):
            ax[q, yy] = pair(q, yy, 0, 1 - x)
        send(ax.at[q], axr.at[q], rs.at[q, 0], rr_.at[q, 0], *near_x)
        for xx in range(ratio):
            ay[q, xx] = pair(q, 1 - h, 1, xx)
        send(ay.at[q], ayr.at[q], rs.at[q, 1], rr_.at[q, 1], *near_y)
    for q in range(2):
        arrived(axr.at[q], rr_.at[q, 0])
        bx[q] = pair(q, 1 - h, 0, x) + axr[q, 1 - h]
        send(bx.at[q], bxr.at[q], rs.at[q, 2], rr_.at[q, 2], *near_y)
        arrived(ayr.at[q], rr_.at[q, 1])
        by[q] = pair(q, h, 1, 1 - x) + ayr[q, 1 - x]
        send(by.at[q], byr.at[q], rs.at[q, 3], rr_.at[q, 3], *near_x)

    def swap(q, j):
        return copy(
            st.at[pl.ds(j * cols + q * fine, fine)], xr.at[x, pl.ds(q * fine, fine)],
            xs.at[q, j], xrs.at[q, x], z, r * ratio + j,
        )

    for q in range(2):
        low, high = slice(q * fine, (q + 1) * fine), slice(cols + q * fine, cols + (q + 1) * fine)
        arrived(bxr.at[q], rr_.at[q, 2])
        st[low] = pair(q, h, 0, x) + axr[q, h] + bxr[q]
        arrived(byr.at[q], rr_.at[q, 3])
        st[high] = pair(q, h, 1, x) + ayr[q, x] + byr[q]
        for j in range(ratio):
            @pl.when((r != z) | (x != j))
            def _(q=q, j=j):
                swap(q, j).start()

        @pl.when(r == z)
        def _(q=q, low=low):
            xr[x, low] = st[pl.ds(pl.multiple_of(x * cols + q * fine, fine), fine)]

    lane = lax.broadcasted_iota(jnp.int32, (1, LANES), 1)
    group = LANES // own

    def energy(rr, first):
        out = jnp.zeros((1, LANES), jnp.float32)
        for j in range(group):
            at = first + j
            row = pb[at // ratio, pl.ds(rr * ratio + at % ratio, 1)]
            out = jnp.where(lane // own == j, row, out)
        return jnp.broadcast_to(out, (LANES, LANES))

    col_energy = energy(z, x * group).T
    bottom = [col_energy + energy(r, j * group) for j in range(ratio)]
    top = [st[j * cols:(j + 1) * cols].T for j in range(ratio)]

    def share(q):
        part = slice(q * fine, (q + 1) * fine)
        for xx in range(ratio):
            @pl.when((r != z) | (x != xx))
            def _(xx=xx):
                arrived(xr.at[xx, pl.ds(q * fine, fine)], xrs.at[q, xx])

        for j in range(ratio):
            tb[r, x, j, part] = -(top[j][part] + xr[j, part]) / bottom[j][part]
        for way, near in enumerate((near_x, near_y, (near_y[0], near_x[1]))):
            send(tile(r, x, q), tile(r, x, q), ts.at[q, way], tr.at[q, way], *near)
        relay(r, x, q, 0)

    def tile(row, xx, q):
        return tb.at[row, xx, :, pl.ds(q * fine, fine)]

    def relay(row, xx, q, i):
        send(tile(row, xx, q), tile(row, xx, q), us.at[q, i], ur.at[q, i], mate, c)

    def collect(q):
        for way, (row, xx) in enumerate(((r, 1 - x), (near_y[0], x), (near_y[0], 1 - x))):
            arrived(tile(row, xx, q), tr.at[q, way])
            relay(row, xx, q, 1 + way)

    def finish(q):
        other = near_y[0] + mate - r
        for i, (row, xx) in enumerate(((mate, x), (mate, 1 - x), (other, x), (other, 1 - x))):
            arrived(tile(row, xx, q), ur.at[q, i])

    def home(q):
        return copy(db.at[q], o_ref.at[q], ds_.at[q], dr.at[q], z, goal * ratio + x)

    def terms(q, picked):
        part = slice(q * fine, (q + 1) * fine)
        d = None
        for row in picked:
            block = jnp.concatenate([
                jnp.concatenate([tb[row, xx, j, part] for j in range(ratio)], axis=1) for xx in range(ratio)
            ], axis=0)
            term = dot3(halves(block), fac(row), NN)
            d = term if d is None else d + term
        return d

    def density(q):
        d = terms(q, (r, near_y[0]))
        finish(q)
        d = d + terms(q, (mate, near_y[0] + mate - r))
        db[q, :LANES] = d[:, :LANES].T
        db[q, LANES:] = d[:, LANES:].T

        @pl.when(~stays)
        def _():
            home(q).start()

        @pl.when(stays)
        def _():
            o_ref[q] = db[q]

    share(0)
    share(1)
    collect(0)
    density(0)
    collect(1)
    for j in range(ratio):
        t_ref[j * cols:(j + 1) * cols] = tb[r, x, j].T
    density(1)

    for cp in pending:
        cp.wait_send()
    for s in range(n_z - 1):
        for off in group8 + [None]:
            for go, make in hops(s, off):
                @pl.when(go)
                def _(make=make):
                    make().wait_send()
    for q in range(2):
        for j in range(ratio):
            @pl.when((r != z) | (x != j))
            def _(q=q, j=j):
                swap(q, j).wait_send()

    @pl.when(~stays)
    def _():
        for q in range(2):
            home(q).wait_send()
            home(q).wait_recv()


def settle(new_ref, turned_ref, new_out, turned_out):
    new_out[...] = new_ref[...]
    low, high = turned_ref[0], turned_ref[1]
    half = low.shape[1] // 2
    turned_out[:, :2 * half] = jnp.concatenate([low[:, :half], high[:, :half]], axis=1)
    turned_out[:, 2 * half:] = jnp.concatenate([low[:, half:], high[:, half:]], axis=1)


def fits(mesh, rows, cols, own, width):
    n_row, n_col = mesh.shape["row"], mesh.shape["col"]
    ratio = n_col // n_row
    return (
        n_col == ratio * n_row and n_col == SUB and ratio == 2 and n_row == 4
        and rows == ratio * cols and cols == LANES
        and rows == n_col * own and LANES % own == 0 and own % (4 * SUB) == 0
        and 2 * width == 3 * LANES and 60 * rows * rows * n_row <= 64 * 2**20
    )


def fused(n_row, ratio, amplitudes, factors, occ_map, vir_map, occ_energy, vir_energy):
    rows, cols = amplitudes.shape
    own, n_aux = factors.shape
    n_col = n_row * ratio
    width = n_aux // n_col
    n_h = n_row // 2
    peers = n_h * ratio - 1
    deep = own + own // 2
    f32, bf16 = jnp.float32, jnp.bfloat16
    dma = pltpu.SemaphoreType.DMA
    vmem = pl.BlockSpec(memory_space=pltpu.VMEM)
    fine = cols // 2
    new, turned = pl.pallas_call(
        functools.partial(kernel, n_row, ratio, own, width),
        out_shape=(
            pltpu.VMEM((rows, cols), f32),
            pltpu.VMEM((2, width, cols), f32),
        ),
        in_specs=[pl.BlockSpec(memory_space=pltpu.HBM)] * 6,
        out_specs=(vmem, vmem),
        scratch_shapes=[
            pltpu.VMEM(factors.shape, f32),
            pltpu.VMEM((rows, cols), f32),
            pltpu.VMEM((1, own), jnp.int32),
            pltpu.VMEM((1, own), jnp.int32),
            pltpu.VMEM((1,) + occ_energy.shape, f32),
            pltpu.VMEM((1,) + vir_energy.shape, f32),
            pltpu.VMEM((n_col, deep, LANES), f32),
            pltpu.VMEM((n_col, SUB, LANES), f32),
            pltpu.VMEM((n_row, SUB, LANES), f32),
            pltpu.VMEM((n_row, n_row, ratio, deep, LANES), f32),
            pltpu.VMEM((n_row, rows, width), bf16),
            pltpu.VMEM((n_row, rows, width), bf16),
            pltpu.VMEM((n_row, ratio, cols, rows), f32),
            pltpu.VMEM((2, n_h, ratio, ratio, fine, cols), f32),
            pltpu.VMEM((2, n_h, ratio, ratio, fine, cols), f32),
            pltpu.VMEM((2, n_h, ratio, ratio, fine, cols), f32),
            pltpu.VMEM((2, n_h, fine, cols), f32),
            pltpu.VMEM((2, n_h, fine, cols), f32),
            pltpu.VMEM((2, ratio, fine, cols), f32),
            pltpu.VMEM((2, ratio, fine, cols), f32),
            pltpu.VMEM((2, fine, cols), f32),
            pltpu.VMEM((2, fine, cols), f32),
            pltpu.VMEM((2, fine, cols), f32),
            pltpu.VMEM((2, fine, cols), f32),
            pltpu.VMEM((rows, cols), f32),
            pltpu.VMEM((ratio, cols, cols), f32),
            pltpu.VMEM((n_row, ratio, ratio, cols, cols), f32),
            pltpu.VMEM((ratio, cols, width), f32),
            pltpu.VMEM((2, width, cols), f32),
            dma((6,)),
            dma((n_col - 1,)), dma((n_col,)),
            dma((n_col - 1,)), dma((n_col,)),
            dma((2, n_row, n_col + 1)), dma((n_row, n_col + 1)),
            dma((peers,)), dma((n_h, ratio)),
            dma((peers + 1,)), dma((n_h, ratio)),
            dma((2,)), dma((2,)),
            dma((2, 4)), dma((2, 4)),
            dma((2, ratio)), dma((2, ratio)),
            dma((2, 3)), dma((2, 3)),
            dma((2, 4)), dma((2, 4)),
            dma((2,)), dma((2,)),
        ],
        compiler_params=pltpu.CompilerParams(
            collective_id=0, has_side_effects=True, vmem_limit_bytes=32 * 2**20
        ),
    )(
        *(pltpu.with_memory_space_constraint(v, pltpu.HBM) for v in (
            factors, amplitudes, occ_map[None, :], vir_map[None, :], occ_energy[None, :], vir_energy[None, :]
        ))
    )
    new, turned = pl.pallas_call(
        settle,
        out_shape=(
            jax.ShapeDtypeStruct((rows, cols), f32),
            jax.ShapeDtypeStruct((width, rows), f32),
        ),
        in_specs=[vmem, vmem],
        out_specs=(vmem, vmem),
        compiler_params=pltpu.CompilerParams(vmem_limit_bytes=4 * 2**20),
    )(new, turned)
    return new, turned.T


def solution(mesh):
    n_row, n_col = mesh.shape["row"], mesh.shape["col"]

    def per_device(amplitudes, factors, *rest):
        rows, cols = amplitudes.shape
        own, n_aux = factors.shape
        if fits(mesh, rows, cols, own, n_aux // n_col):
            return fused(n_row, n_col // n_row, amplitudes, factors, *rest)
        return general(amplitudes, factors, *rest)

    placed = (
        P("row", "col"),
        P(("row", "col"), None),
        P(("row", "col")),
        P(("row", "col")),
        P(),
        P(),
    )
    return jax.shard_map(
        per_device,
        mesh=mesh,
        in_specs=placed,
        out_specs=(P("row", "col"), P("row", "col")),
        check_vma=False,
    )
```
